256 devices in a mesh: section: 8 (over x, core), seq: 32 (over z, y).
Axes of the slice: x: 4, y: 4, z: 8, core: 2. Of those that a mesh axis runs over, the one named last changes fastest.
Arguments:
- query: bfloat16 [8, 16384, 1024], P('section', 'seq'), may hold values from -6 to 6
- key: bfloat16 [8, 16384, 1024], P('section', 'seq'), may hold values from -6 to 6
- value: bfloat16 [8, 16384, 1024], P('section', 'seq'), may hold values from -6 to 6
- grad_sent: bfloat16 [8, 16384, 2048], P('section', 'seq'), may hold values from -6 to 6
- out_weight: bfloat16 [8, 1024, 2048], P('section'), may hold values from -0.125 to 0.125
- assign: int32 [8, 4, 16384], P('section', None, 'seq'), may hold values from 0 to 7, as said below
Outputs:
- grad_query: bfloat16 [8, 16384, 1024], P('section', 'seq')
- grad_key: bfloat16 [8, 16384, 1024], P('section', 'seq')
- grad_value: bfloat16 [8, 16384, 1024], P('section', 'seq')
The draws below stay inside these ranges and needn't reach their ends.
Inputs may be any that keep to these rules, and one draw needn't show every extreme that they name: `assign`: for each section and routing head, every cluster holds exactly 2048 tokens. The 512 tokens of one device put 1, 3, 5 or 7 times 112 // 7 tokens into one cluster, so at most 112, and some device reaches 112 for every section and head.
All inputs are finite; a program needn't handle non-finite values.
Results may differ from the reference program's by a relative error of at most 0.0058.
Values may be sent and summed in bfloat16 or wider, within the bound.
A program may use at most 128 MiB of HBM per device.

```python
import jax
import jax.numpy as jnp
from jax import lax

D = 2048
HR = 4
HL = 4
HD = 128
CS = 2048
WIN = 512
TOK_DEV = 512
SECTIONS = 8
TOKENS = 16384
NCL = 8
HH = 1024


def balanced_assign(key):
    devices = TOKENS // TOK_DEV
    clusters = TOKENS // CS
    average = CS // devices
    slots = jnp.arange(TOK_DEV, dtype=jnp.int32)

    def one_head(head_key):
        parts = jax.random.split(head_key, 3)
        device_order = jax.random.permutation(parts[0], devices).astype(jnp.int32)
        cluster_order = jax.random.permutation(parts[1], clusters).astype(jnp.int32)
        first_sign = 1 - 2 * (device_order % 2)
        second_sign = 1 - 2 * (device_order // 2 % 2)
        column_sign = 1 - 2 * (cluster_order % 2)
        counts = average + column_sign[None, :] * (first_sign[:, None] * (average // 2) + second_sign[:, None] * (average // 4))
        bounds = jnp.cumsum(counts, axis=1).astype(jnp.int32)
        labels = jax.vmap(lambda edge: jnp.searchsorted(edge, slots, side='right'))(bounds).astype(jnp.int32)
        shuffles = jax.vmap(lambda part_key: jax.random.permutation(part_key, TOK_DEV))(jax.random.split(parts[2], devices)).astype(jnp.int32)
        device_rows = jnp.arange(devices, dtype=jnp.int32)[:, None]
        placed = jnp.zeros((devices, TOK_DEV), jnp.int32).at[device_rows, shuffles].set(labels)
        return placed.reshape(TOKENS)
    head_keys = jax.random.split(jax.random.fold_in(key, 17), SECTIONS * HR)
    return jax.vmap(one_head)(head_keys).reshape(SECTIONS, HR, TOKENS)


def base_values(key, salt):
    shape = (SECTIONS, TOKENS, HR + HL, HD)
    values = jax.random.truncated_normal(jax.random.fold_in(key, salt), -6.0, 6.0, shape, jnp.float32)
    return values


def draw_assign(key, part):
    return balanced_assign(key)


def draw_query(key, part):
    values = base_values(key, 1)
    return values.reshape(SECTIONS, TOKENS, (HR + HL) * HD).astype(jnp.bfloat16)


def draw_key(key, part):
    values = base_values(key, 2)
    return values.reshape(SECTIONS, TOKENS, (HR + HL) * HD).astype(jnp.bfloat16)


def shard_levels(rng, dims, cuts, low, high):
    level = 1.0
    for dim, blocks in cuts:
        steps = jax.random.uniform(jax.random.fold_in(jax.random.fold_in(rng, 6), dim), (blocks,), jnp.float32, low / len(cuts), high / len(cuts))
        level = level * jnp.repeat(jnp.exp(steps), dims[dim] // blocks).reshape((-1,) + (1,) * (len(dims) - 1 - dim))
    return level


def scatter_about(stream_key, extent, spread, most, cuts=(), kind=jnp.bfloat16):
    level = shard_levels(stream_key, extent, cuts, -0.22, 0.18) if cuts else 1.0
    values = jax.random.normal(stream_key, extent, jnp.float32) * spread * level
    return jnp.minimum(jnp.maximum(values, -most), most).astype(kind)


def setup_inputs(seed: int = 0) -> dict:
    key_list = jax.random.split(jax.random.key(seed), 7)
    query = draw_query(jax.random.fold_in(key_list[6], 71), 0)
    key = draw_key(jax.random.fold_in(key_list[6], 71), 0)
    value = scatter_about(key_list[2], (SECTIONS, TOKENS, HH), 1.0, 6.0, ((0, 8), (1, 32)))
    grad_sent = scatter_about(key_list[3], (SECTIONS, TOKENS, D), 1.0, 6.0, ((0, 8), (1, 32)))
    out_weight = scatter_about(key_list[4], (SECTIONS, HH, D), D ** -0.5, 0.125, ((0, 8),))
    assign = draw_assign(jax.random.fold_in(key_list[6], 71), 0)
    return dict(query=query, key=key, value=value, grad_sent=grad_sent, out_weight=out_weight, assign=assign)


def cluster_block(query_rows, key_rows, value_rows, grad_rows, allowed, factor):
    scores = jnp.dot(query_rows, key_rows.T, preferred_element_type=jnp.float32) * factor
    scores = jnp.where(allowed, scores, -1e30)
    highest = jnp.max(scores, axis=1, keepdims=True)
    weights = jnp.exp(scores - highest)
    probs = weights / jnp.sum(weights, axis=1, keepdims=True)
    dprob = jnp.dot(grad_rows, value_rows.T, preferred_element_type=jnp.float32)
    delta = jnp.sum(probs * dprob, axis=1, keepdims=True)
    dscore = probs * (dprob - delta)
    probs_b = probs.astype(jnp.bfloat16)
    dscore_b = dscore.astype(jnp.bfloat16)
    grad_query = jnp.dot(dscore_b, key_rows, preferred_element_type=jnp.float32) * factor
    grad_key = jnp.dot(dscore_b.T, query_rows, preferred_element_type=jnp.float32) * factor
    grad_value = jnp.dot(probs_b.T, grad_rows, preferred_element_type=jnp.float32)
    return grad_query, grad_key, grad_value


def cluster_grads(query_rows, key_rows, value_rows, grad_rows, factor):
    length = query_rows.shape[0]
    span = min(512, length)
    pieces = []
    total_key = jnp.zeros(key_rows.shape, jnp.float32)
    total_value = jnp.zeros(value_rows.shape, jnp.float32)
    for index in range(length // span):
        first = index * span
        end = first + span
        allowed = jnp.arange(end, dtype=jnp.int32)[None, :] <= (first + jnp.arange(span, dtype=jnp.int32))[:, None]
        part_query, part_key, part_value = cluster_block(query_rows[first:end], key_rows[:end], value_rows[:end], grad_rows[first:end], allowed, factor)
        pieces.append(part_query)
        total_key = total_key.at[:end].add(part_key)
        total_value = total_value.at[:end].add(part_value)
    return jnp.concatenate(pieces, axis=0), total_key, total_value


def window_block(query_rows, key_rows, value_rows, grad_rows, allowed, factor):
    query_float = query_rows.astype(jnp.float32)
    key_float = key_rows.astype(jnp.float32)
    value_float = value_rows.astype(jnp.float32)
    grad_float = grad_rows.astype(jnp.float32)
    scores = jnp.einsum('qhd,khd->hqk', query_float, key_float) * factor
    scores = jnp.where(allowed[None], scores, -1e30)
    highest = jnp.max(scores, axis=2, keepdims=True)
    weights = jnp.exp(scores - highest)
    probs = weights / jnp.sum(weights, axis=2, keepdims=True)
    dprob = jnp.einsum('qhd,khd->hqk', grad_float, value_float)
    delta = jnp.sum(probs * dprob, axis=2, keepdims=True)
    dscore = probs * (dprob - delta)
    probs_b = lax.optimization_barrier(probs.astype(jnp.bfloat16)).astype(jnp.float32)
    dscore_b = lax.optimization_barrier(dscore.astype(jnp.bfloat16)).astype(jnp.float32)
    grad_query = jnp.einsum('hqk,khd->qhd', dscore_b, key_float) * factor
    grad_key = jnp.einsum('hqk,qhd->khd', dscore_b, query_float) * factor
    grad_value = jnp.einsum('hqk,qhd->khd', probs_b, grad_float)
    return grad_query, grad_key, grad_value


def section_grads(operands):
    query, key, value, boundary, weight, labels = operands
    factor = HD ** -0.5
    heads = HR + HL
    attn_grad = jnp.dot(boundary, weight.T, preferred_element_type=jnp.float32).astype(jnp.bfloat16)
    query_heads = query.reshape(TOKENS, heads, HD)
    key_heads = key.reshape(TOKENS, heads, HD)
    value_heads = value.reshape(TOKENS, heads, HD)
    grad_heads = attn_grad.reshape(TOKENS, heads, HD)
    positions = jnp.arange(TOKENS, dtype=jnp.int32)
    routed = ([], [], [])
    for head in range(HR):
        order = jnp.argsort(labels[head] * TOKENS + positions).astype(jnp.int32)

        def grouped(array):
            return array[order, head].reshape(NCL, CS, HD)

        results = lax.map(lambda group: cluster_grads(group[0], group[1], group[2], group[3], factor),
                          (grouped(query_heads), grouped(key_heads), grouped(value_heads), grouped(grad_heads)))
        for bucket, result in zip(routed, results):
            placed = jnp.zeros((TOKENS, HD), jnp.bfloat16).at[order].set(result.astype(jnp.bfloat16).reshape(TOKENS, HD))
            bucket.append(placed)
    local_query = query_heads[:, HR:]
    local_key = key_heads[:, HR:]
    local_value = value_heads[:, HR:]
    local_grad = grad_heads[:, HR:]
    padding = jnp.zeros((WIN, HL, HD), local_key.dtype)
    keys_padded = jnp.concatenate([padding, local_key], axis=0)
    values_padded = jnp.concatenate([padding, local_value], axis=0)
    span = min(512, TOK_DEV)

    def local_step(carry, index):
        total_key, total_value = carry
        first = index * span
        query_rows = lax.dynamic_slice_in_dim(local_query, first, span, 0)
        grad_rows = lax.dynamic_slice_in_dim(local_grad, first, span, 0)
        key_rows = lax.dynamic_slice_in_dim(keys_padded, first, span + WIN, 0)
        value_rows = lax.dynamic_slice_in_dim(values_padded, first, span + WIN, 0)
        query_pos = first + jnp.arange(span, dtype=jnp.int32)
        key_pos = first - WIN + jnp.arange(span + WIN, dtype=jnp.int32)
        allowed = (key_pos[None, :] > query_pos[:, None] - WIN) & (key_pos[None, :] <= query_pos[:, None]) & (key_pos[None, :] >= 0)
        part_query, part_key, part_value = window_block(query_rows, key_rows, value_rows, grad_rows, allowed, factor)
        total_key = lax.dynamic_update_slice_in_dim(total_key, lax.dynamic_slice_in_dim(total_key, first, span + WIN, 0) + part_key, first, 0)
        total_value = lax.dynamic_update_slice_in_dim(total_value, lax.dynamic_slice_in_dim(total_value, first, span + WIN, 0) + part_value, first, 0)
        return (total_key, total_value), part_query

    empty = jnp.zeros((TOKENS + WIN, HL, HD), jnp.float32)
    (total_key, total_value), local_dq = lax.scan(local_step, (empty, empty), jnp.arange(TOKENS // span, dtype=jnp.int32))
    local_dq = local_dq.reshape(TOKENS, HL, HD).astype(jnp.bfloat16)
    local_dk = total_key[WIN:].astype(jnp.bfloat16)
    local_dv = total_value[WIN:].astype(jnp.bfloat16)
    out_query = jnp.concatenate([jnp.stack(routed[0], axis=1), local_dq], axis=1).reshape(TOKENS, heads * HD)
    out_key = jnp.concatenate([jnp.stack(routed[1], axis=1), local_dk], axis=1).reshape(TOKENS, heads * HD)
    out_value = jnp.concatenate([jnp.stack(routed[2], axis=1), local_dv], axis=1).reshape(TOKENS, heads * HD)
    return out_query, out_key, out_value


def reference(query, key, value, grad_sent, out_weight, assign):
    boundary = jnp.roll(grad_sent, -1, axis=0)
    grad_query, grad_key, grad_value = lax.map(section_grads, (query, key, value, boundary, out_weight, assign))
    return grad_query, grad_key, grad_value
```

```python
import functools

import jax
import jax.numpy as jnp
from jax import lax
from jax.experimental import pallas as pl
from jax.experimental.pallas import tpu as pltpu
from jax.sharding import PartitionSpec as P

MESH = pl.DeviceIdType.MESH
BF = jnp.bfloat16
F32 = jnp.float32
I32 = jnp.int32
HR = 4
HD = 128
FACTOR = HD ** (-0.5)
NT = (((1,), (1,)), ((), ()))


def remote(src, dst, send, recv, device):
    return pltpu.make_async_remote_copy(
        src_ref=src, dst_ref=dst, send_sem=send, recv_sem=recv, device_id=device, device_id_type=MESH
    )


def place():
    sec = lax.axis_index("section")
    me = lax.axis_index("seq")
    return sec, me, (sec // 2) * 2, sec % 2, me // 4, me % 4


def plane_barrier(outside):
    sec, me, base, core, z, y = place()
    barrier = pltpu.get_barrier_semaphore()
    mine = core * 32 + me

    def greet(step, carry):
        other = (mine + step) % 64
        pl.semaphore_signal(
            barrier, inc=1, device_id=(base + other // 32, other % 32), device_id_type=MESH
        )
        return carry

    lax.fori_loop(1, 64, greet, 0)
    if outside:
        pl.semaphore_signal(
            barrier, inc=1, device_id=((sec + 2 * core + 7) % 8, me), device_id_type=MESH
        )
    pl.semaphore_wait(barrier, 64 if outside else 63)


def forward_kernel(
    q, k, v, grad_hbm, weight_hbm, rank_row, tiles,
    comp, grad_heads, halo_k, halo_v, tab,
    grad_in, weight, dense, mid0, mid1, mid2, mid3, pick, spread, arr0, arr1, arr2, arr3, counts, table,
    send_count, recv_count, send_grad, recv_grad, weight_sem, send_one, recv_one, send_two, recv_two,
    send_halo, recv_halo, table_sem,
):
    sec, me, base, core, z, y = place()
    seat = y * 2 + core
    parity = z % 2
    mid = (mid0, mid1, mid2, mid3)
    arrived = (arr0, arr1, arr2, arr3)
    get_weight = pltpu.make_async_copy(weight_hbm, weight, weight_sem)
    get_weight.start()
    plane_barrier(True)

    def count_copy(n):
        plane = 2 * (n // 8) + core
        dest_section = base + n % 2
        dest = plane * 4 + (n % 8) // 2
        own = (dest_section == sec) & (dest == me)
        copy = remote(
            tiles.at[n // 8], counts.at[me], send_count.at[n], recv_count, (dest_section, dest)
        )
        return own, copy

    def send_counts(n, carry):
        own, copy = count_copy(n)

        @pl.when(own)
        def _():
            pltpu.make_async_copy(tiles.at[n // 8], counts.at[me], recv_count).start()

        @pl.when(jnp.logical_not(own))
        def _():
            copy.start()

        return carry

    lax.fori_loop(0, 32, send_counts, 0)
    grad_copy = remote(grad_hbm, grad_in, send_grad, recv_grad, ((sec + 7) % 8, me))
    grad_copy.start()
    after = (sec, (me + 1) % 32)
    halo_copies = [
        remote(src.at[:, pl.ds(512, 512)], dst, send_halo.at[n], recv_halo.at[n], after)
        for n, (src, dst) in enumerate(((k, halo_k), (v, halo_v)))
    ]

    def one_copy(t, h):
        return remote(
            dense.at[t, h], mid[t].at[z // 2], send_one.at[t, h], recv_one.at[t, z // 2],
            (base + parity, (2 * h + core) * 4 + y),
        )

    def start_one(t, h):
        own = (2 * h + core) == z

        @pl.when(own)
        def _():
            pltpu.make_async_copy(dense.at[t, h], mid[t].at[z // 2], recv_one.at[t, z // 2]).start()

        @pl.when(jnp.logical_not(own))
        def _():
            one_copy(t, h).start()

    rows = lax.broadcasted_iota(I32, (512, 512), 0)
    for h in range(HR):
        pick[h] = jnp.where(rows == rank_row[h : h + 1, :], 1.0, 0.0).astype(BF)
    for t, src in enumerate((k, v, q)):
        for h in range(HR):
            rowsh = jnp.dot(pick[h], src[:, h * HD : (h + 1) * HD], preferred_element_type=F32)
            dense[t, h] = rowsh.astype(BF).reshape(32, 16, HD)
            start_one(t, h)
        if t == 0:
            for copy in halo_copies:
                copy.start()

    pltpu.make_async_copy(counts, counts, recv_count).wait()
    tab[0:32, :] = counts[:, 1, :]
    tab[72:104, :] = counts[:, 2, :]
    unit = counts[:, 0, :].astype(F32)
    below = (
        lax.broadcasted_iota(I32, (32, 32), 0) >= lax.broadcasted_iota(I32, (32, 32), 1)
    ).astype(F32)
    ends = jnp.dot(below, unit, preferred_element_type=F32)
    lane = lax.broadcasted_iota(I32, (32, 128), 1)
    mine = lane == seat
    my_end = jnp.sum(jnp.where(mine, ends, 0.0), axis=1, keepdims=True)
    my_unit = jnp.sum(jnp.where(mine, unit, 0.0), axis=1, keepdims=True)
    tab[32:64, :] = jnp.broadcast_to(my_end - my_unit, (32, 128)).astype(I32)
    passed = jnp.broadcast_to(my_end, (32, 128)) <= lane.astype(F32)
    source = jnp.sum(jnp.where(passed, 1.0, 0.0), axis=0, keepdims=True).astype(I32)
    begin = jnp.sum(jnp.where(passed, my_unit, 0.0), axis=0, keepdims=True).astype(I32)
    inside = lax.broadcasted_iota(I32, (1, 128), 1) - begin
    sz = source >> 2
    address = ((source & 3) * 2 + (sz & 1)) * 28 + (sz >> 1) * 7 + inside
    tab[64:72, :] = jnp.broadcast_to(address, (8, 128))
    table_copy = pltpu.make_async_copy(tab, table, table_sem)
    table_copy.start()
    table_copy.wait()

    def two_copy(t, d):
        c = (seat + d) % 8
        return remote(
            spread.at[t, d], arrived[t].at[pl.ds(seat * 28, 28)], send_two.at[t, d],
            recv_two.at[t, seat], (base + c % 2, z * 4 + c // 2),
        )

    def second_stage(t):
        for slot in range(4):
            remote(
                mid[t].at[slot], mid[t].at[slot], send_one.at[t, 0], recv_one.at[t, slot], (sec, me)
            ).wait_recv()

        def expand(d):
            c = (seat + d) % 8
            for slot in range(4):
                first = table[(slot * 2 + core) * 4 + y, c]
                for r in range(7):
                    spread[t, d, slot * 7 + r] = mid[t][slot, jnp.clip(first + r, 0, 31)]

        def step(d, carry):
            expand(d)
            two_copy(t, d).start()
            return carry

        lax.fori_loop(1, 8, step, 0)
        expand(0)
        pltpu.make_async_copy(
            spread.at[t, 0], arrived[t].at[pl.ds(seat * 28, 28)], recv_two.at[t, seat]
        ).start()

    second_stage(0)
    grad_copy.wait_recv()
    get_weight.wait()

    def project(n, carry):
        part = lax.dot_general(
            grad_in[...], weight[pl.ds(pl.multiple_of(n * 256, 256), 256), :], NT,
            preferred_element_type=F32,
        ).astype(BF)
        grad_heads[2 * n] = part[:, :HD]
        grad_heads[2 * n + 1] = part[:, HD:]
        return carry

    lax.fori_loop(0, 4, project, 0)
    for h in range(HR):
        rowsh = jnp.dot(pick[h], grad_heads[h], preferred_element_type=F32)
        dense[3, h] = rowsh.astype(BF).reshape(32, 16, HD)
        start_one(3, h)
    second_stage(1)
    second_stage(2)
    second_stage(3)
    for t in range(4):
        def await_two(j, carry, t=t):
            region = arrived[t].at[pl.ds(j * 28, 28)]
            remote(region, region, send_two.at[t, 0], recv_two.at[t, j], (sec, me)).wait_recv()
            return carry

        lax.fori_loop(0, 8, await_two, 0)

        def gather(n, carry, t=t):
            for m in range(8):
                comp[t, n * 8 + m] = arrived[t][jnp.clip(table[64, n * 8 + m], 0, 223)]
            return carry

        lax.fori_loop(0, 16, gather, 0)
    for copy in halo_copies:
        copy.wait()
    grad_copy.wait_send()

    def drain_counts(n, carry):
        own, copy = count_copy(n)

        @pl.when(jnp.logical_not(own))
        def _():
            copy.wait_send()

        return carry

    lax.fori_loop(0, 32, drain_counts, 0)
    for t in range(4):
        for h in range(HR):
            @pl.when((2 * h + core) != z)
            def _(t=t, h=h):
                one_copy(t, h).wait_send()

        def drain_two(d, carry, t=t):
            two_copy(t, d).wait_send()
            return carry

        lax.fori_loop(1, 8, drain_two, 0)


def return_kernel(
    answer, carry_grad, table,
    back, carry_in,
    spread, arr0, arr1, arr2, dense,
    send_one, recv_one, send_two, recv_two, send_carry, recv_carry,
):
    sec, me, base, core, z, y = place()
    seat = y * 2 + core
    arrived = (arr0, arr1, arr2)
    plane_barrier(False)
    carry_copy = remote(carry_grad, carry_in, send_carry, recv_carry, (sec, (me + 31) % 32))

    def one_copy(t, d):
        j = (seat + d) % 8
        return remote(
            spread.at[t, d], arrived[t].at[pl.ds(seat * 28, 28)], send_one.at[t, d],
            recv_one.at[t, seat], (base + j % 2, z * 4 + j // 2),
        )

    def expand(t, d):
        j = (seat + d) % 8
        for slot in range(4):
            first = table[32 + (slot * 2 + j % 2) * 4 + j // 2, 0]
            for r in range(7):
                spread[t, d, slot * 7 + r] = answer[t, jnp.clip(first + r, 0, 127)]

    for t in range(3):
        def step(d, carry, t=t):
            expand(t, d)
            one_copy(t, d).start()
            return carry

        lax.fori_loop(1, 8, step, 0)
        expand(t, 0)
        pltpu.make_async_copy(
            spread.at[t, 0], arrived[t].at[pl.ds(seat * 28, 28)], recv_one.at[t, seat]
        ).start()

    carry_copy.start()

    def two_copy(t, slot):
        return remote(
            dense.at[t, slot], back.at[t, z // 2], send_two.at[t, slot], recv_two.at[t, z // 2],
            (base + z % 2, (slot * 2 + core) * 4 + y),
        )

    def own_slot(slot):
        return ((slot * 2 + core) == z) & (z % 2 == core)

    for t in range(3):
        def await_one(j, carry, t=t):
            region = arrived[t].at[pl.ds(j * 28, 28)]
            remote(region, region, send_one.at[t, 0], recv_one.at[t, j], (sec, me)).wait_recv()
            return carry

        lax.fori_loop(0, 8, await_one, 0)
        for slot in range(4):
            row = 72 + (slot * 2 + core) * 4 + y

            def gather(n, carry, t=t, slot=slot, row=row):
                for m in range(8):
                    dense[t, slot, n * 8 + m] = arrived[t][jnp.clip(table[row, n * 8 + m] + slot * 7, 0, 223)]
                return carry

            lax.fori_loop(0, 4, gather, 0)

            @pl.when(own_slot(slot))
            def _(t=t, slot=slot):
                pltpu.make_async_copy(
                    dense.at[t, slot], back.at[t, z // 2], recv_two.at[t, z // 2]
                ).start()

            @pl.when(jnp.logical_not(own_slot(slot)))
            def _(t=t, slot=slot):
                two_copy(t, slot).start()

    for t in range(3):
        for h in range(HR):
            remote(
                back.at[t, h], back.at[t, h], send_two.at[t, 0], recv_two.at[t, h], (sec, me)
            ).wait_recv()
    carry_copy.wait()
    for t in range(3):
        def drain(d, carry, t=t):
            one_copy(t, d).wait_send()
            return carry

        lax.fori_loop(1, 8, drain, 0)
        for slot in range(4):
            @pl.when(jnp.logical_not(own_slot(slot)))
            def _(t=t, slot=slot):
                two_copy(t, slot).wait_send()


def block_rows(ref, index, first, count):
    return ref[index, pl.ds(first, count), :]


def attend(score, dprob, q_blk, g_blk, key_of, value_of, flip_of, masks, add):
    count = len(masks)
    top = None
    for n in range(count):
        s = lax.dot_general(key_of(n), q_blk, NT, preferred_element_type=F32) * FACTOR
        if masks[n] is not None:
            s = jnp.where(masks[n], s, -1e30)
        score[n] = s
        high = jnp.max(s, axis=0, keepdims=True)
        top = high if top is None else jnp.maximum(top, high)
    total = jnp.zeros((1, 256), F32)
    cross = jnp.zeros((1, 256), F32)
    for n in range(count):
        e = jnp.exp(score[n] - top)
        dp = lax.dot_general(value_of(n), g_blk, NT, preferred_element_type=F32)
        score[n] = e
        dprob[n] = dp
        total = total + jnp.sum(e, axis=0, keepdims=True)
        cross = cross + jnp.sum(e * dp, axis=0, keepdims=True)
    inverse = 1.0 / total
    delta = cross * inverse
    flipped = jnp.zeros((HD, 256), F32)
    for n in range(count):
        prob = score[n] * inverse
        ds = (prob * (dprob[n] - delta)).astype(BF)
        add(n, jnp.dot(ds, q_blk, preferred_element_type=F32),
            jnp.dot(prob.astype(BF), g_blk, preferred_element_type=F32))
        flipped = flipped + jnp.dot(flip_of(n), ds, preferred_element_type=F32)
    return (jnp.transpose(flipped) * FACTOR).astype(BF)


def compute_kernel(
    comp, q, k, v, grad_heads, halo_k, halo_v,
    answer, local_q, local_k, local_v, carry_grad,
    score, dprob, flip, total_k, total_v,
):
    me = lax.axis_index("seq")
    low = lax.broadcasted_iota(I32, (256, 256), 0)
    col = lax.broadcasted_iota(I32, (256, 256), 1)
    total_k[...] = jnp.zeros_like(total_k)
    total_v[...] = jnp.zeros_like(total_v)
    for n in range(8):
        flip[n] = jnp.transpose(comp[0, n * 256 : (n + 1) * 256, :].astype(F32)).astype(BF)
    causal = low <= col
    for blk in range(7, -1, -1):
        rows = slice(blk * 256, (blk + 1) * 256)

        def add(n, dk, dv):
            total_k[n * 256 : (n + 1) * 256, :] += dk
            total_v[n * 256 : (n + 1) * 256, :] += dv

        answer[2, rows, :] = attend(
            score, dprob, comp[2, rows, :], comp[3, rows, :],
            lambda n: comp[0, n * 256 : (n + 1) * 256, :],
            lambda n: comp[1, n * 256 : (n + 1) * 256, :],
            lambda n: flip[n],
            [None] * blk + [causal], add,
        )
        answer[0, rows, :] = (total_k[rows, :] * FACTOR).astype(BF)
        answer[1, rows, :] = total_v[rows, :].astype(BF)
    first_ok = me > 0
    for h in range(4):
        cols = slice((h + 4) * HD, (h + 5) * HD)
        half = slice(h * HD, (h + 1) * HD)

        def key_rows(n, halo, own):
            return halo[n * 256 : (n + 1) * 256, half] if n < 2 else own[(n - 2) * 256 : (n - 1) * 256, cols]

        for n in range(4):
            flip[n] = jnp.transpose(key_rows(n, halo_k, k).astype(F32)).astype(BF)
        total_k[0:1024, :] = jnp.zeros((1024, HD), F32)
        total_v[0:1024, :] = jnp.zeros((1024, HD), F32)
        for blk in range(2):
            rows = slice(blk * 256, (blk + 1) * 256)
            masks = [low > col, None, low <= col]
            for n in range(3):
                if blk + n < 2:
                    live = jnp.broadcast_to(first_ok, (256, 256))
                    masks[n] = live if masks[n] is None else masks[n] & live

            def add(n, dk, dv, blk=blk):
                spot = slice((blk + n) * 256, (blk + n + 1) * 256)
                total_k[spot, :] += dk
                total_v[spot, :] += dv

            local_q[h, rows, :] = attend(
                score, dprob, q[rows, cols], grad_heads[4 + h, rows, :],
                lambda n: key_rows(blk + n, halo_k, k),
                lambda n: key_rows(blk + n, halo_v, v),
                lambda n: flip[blk + n],
                masks, add,
            )
        carry_grad[0, h] = (total_k[0:512, :] * FACTOR).astype(BF)
        carry_grad[1, h] = total_v[0:512, :].astype(BF)
        local_k[h] = total_k[512:1024, :] * FACTOR
        local_v[h] = total_v[512:1024, :]


def finish_kernel(back, carry_in, rank_col, local_q, local_k, local_v, out_q, out_k, out_v):
    keep = lax.axis_index("seq") < 31
    cols = lax.broadcasted_iota(I32, (512, 512), 1)
    for h in range(HR):
        place_rows = jnp.where(cols == rank_col[:, h : h + 1], 1.0, 0.0).astype(BF)
        span = slice(h * HD, (h + 1) * HD)
        for t, out in enumerate((out_k, out_v, out_q)):
            out[:, span] = jnp.dot(place_rows, back[t, h], preferred_element_type=F32).astype(BF)
        span = slice((h + 4) * HD, (h + 5) * HD)
        out_q[:, span] = local_q[h]
        for t, (out, local) in enumerate(((out_k, local_k), (out_v, local_v))):
            extra = jnp.where(keep, carry_in[t, h].astype(F32), 0.0)
            out[:, span] = (local[h] + extra).astype(BF)


VM = pl.BlockSpec(memory_space=pltpu.VMEM)
SM = pl.BlockSpec(memory_space=pltpu.SMEM)
HBM = pl.BlockSpec(memory_space=pl.ANY)
SDS = jax.ShapeDtypeStruct
DMA = pltpu.SemaphoreType.DMA


def plan(labels):
    members = (labels[:, :, None] == jnp.arange(8, dtype=I32)[None, None, :]).astype(BF)
    ids = jnp.arange(512, dtype=I32)
    lower = (ids[:, None] >= ids[None, :]).astype(BF)
    running = jnp.einsum("ts,hsc->htc", lower, members, preferred_element_type=F32)
    counts = running[:, -1, :].astype(I32)
    clusters = jnp.arange(8, dtype=I32)
    ends = jnp.sum(jnp.where(clusters[:, None] <= clusters[None, :], counts[:, :, None], 0), axis=1)
    starts = ends - counts
    offset = running - 1.0 + starts.astype(F32)[:, None, :]
    ranks = jnp.sum(jnp.where(members > 0, offset, 0.0), axis=2).astype(I32)
    units, unit_start, unit_end = counts // 16, starts // 16, ends // 16
    lanes = jnp.arange(128, dtype=I32)
    passed = unit_end[:, :, None] <= lanes[None, None, :]
    which = jnp.sum(passed.astype(I32), axis=1)
    begun = jnp.sum(jnp.where(passed, units[:, :, None], 0), axis=1)
    inverse = jnp.where(lanes < 32, which * 28 + lanes - begun, 0)
    wide = lambda x: jnp.pad(x, ((0, 0), (0, 120)))
    zero = jnp.zeros_like(inverse)
    tiles = jnp.stack([wide(units), wide(unit_start), inverse] + [zero] * 5, axis=1)
    return ranks, tiles


def body(query, key, value, grad_sent, out_weight, assign):
    ranks, tiles = plan(assign[0])
    rank_row = jnp.pad(ranks, ((0, 4), (0, 0)))
    rank_col = rank_row.T
    q, k, v = query[0], key[0], value[0]
    comp, grad_heads, halo_k, halo_v, tab = pl.pallas_call(
        forward_kernel,
        out_shape=(
            SDS((4, 128, 16, HD), BF), SDS((8, 512, HD), BF), SDS((512, 512), BF),
            SDS((512, 512), BF), SDS((104, 128), I32),
        ),
        in_specs=[VM, VM, VM, HBM, HBM, VM, VM],
        out_specs=(VM, VM, VM, VM, VM),
        scratch_shapes=[
            pltpu.VMEM((512, 2048), BF), pltpu.VMEM((1024, 2048), BF),
            pltpu.VMEM((4, 4, 32, 16, HD), BF), *[pltpu.VMEM((4, 32, 16, HD), BF)] * 4,
            pltpu.VMEM((4, 512, 512), BF), pltpu.VMEM((4, 8, 28, 16, HD), BF),
            *[pltpu.VMEM((224, 16, HD), BF)] * 4, pltpu.VMEM((32, 8, 128), I32),
            pltpu.SMEM((104, 128), I32),
            DMA((32,)), DMA, DMA, DMA, DMA, DMA((4, 4)), DMA((4, 4)), DMA((4, 8)), DMA((4, 8)),
            DMA((2,)), DMA((2,)), DMA,
        ],
        compiler_params=pltpu.CompilerParams(collective_id=0, has_side_effects=True),
        name="exchange_forward",
    )(q, k, v, grad_sent[0], out_weight[0], rank_row, tiles)
    answer, local_q, local_k, local_v, carry_grad = pl.pallas_call(
        compute_kernel,
        out_shape=(
            SDS((3, 2048, HD), BF), SDS((4, 512, HD), BF), SDS((4, 512, HD), F32),
            SDS((4, 512, HD), F32), SDS((2, 4, 512, HD), BF),
        ),
        in_specs=[VM] * 7,
        out_specs=(VM,) * 5,
        scratch_shapes=[
            pltpu.VMEM((8, 256, 256), F32), pltpu.VMEM((8, 256, 256), F32),
            pltpu.VMEM((8, HD, 256), BF), pltpu.VMEM((2048, HD), F32), pltpu.VMEM((2048, HD), F32),
        ],
        name="attention_backward",
    )(comp.reshape(4, 2048, HD), q, k, v, grad_heads, halo_k, halo_v)
    back, carry_in = pl.pallas_call(
        return_kernel,
        out_shape=(SDS((3, 4, 32, 16, HD), BF), SDS((2, 4, 512, HD), BF)),
        in_specs=[VM, VM, SM],
        out_specs=(VM, VM),
        scratch_shapes=[
            pltpu.VMEM((3, 8, 28, 16, HD), BF), *[pltpu.VMEM((224, 16, HD), BF)] * 3,
            pltpu.VMEM((3, 4, 32, 16, HD), BF),
            DMA((3, 8)), DMA((3, 8)), DMA((3, 4)), DMA((3, 4)), DMA, DMA,
        ],
        compiler_params=pltpu.CompilerParams(collective_id=1, has_side_effects=True),
        name="exchange_return",
    )(answer.reshape(3, 128, 16, HD), carry_grad, tab)
    outs = pl.pallas_call(
        finish_kernel,
        out_shape=(SDS((512, 1024), BF),) * 3,
        in_specs=[VM] * 6,
        out_specs=(VM,) * 3,
        name="finish",
    )(back.reshape(3, 4, 512, HD), carry_in, rank_col, local_q, local_k, local_v)
    return tuple(out[None] for out in outs)


def solution(mesh):
    return jax.shard_map(
        body,
        mesh=mesh,
        in_specs=(P("section", "seq", None),) * 4
        + (P("section", None, None), P("section", None, "seq")),
        out_specs=(P("section", "seq", None),) * 3,
        check_vma=False,
    )
```

```python
import functools

import jax
import jax.numpy as jnp
from jax import lax
from jax.experimental import pallas as pl
from jax.experimental.pallas import tpu as pltpu
from jax.sharding import PartitionSpec as P

MESH = pl.DeviceIdType.MESH
BF = jnp.bfloat16
F32 = jnp.float32
I32 = jnp.int32
HR = 4
HD = 128
FACTOR = HD ** (-0.5)
NT = (((1,), (1,)), ((), ()))


def remote(src, dst, send, recv, device):
    return pltpu.make_async_remote_copy(
        src_ref=src, dst_ref=dst, send_sem=send, recv_sem=recv, device_id=device, device_id_type=MESH
    )


def place():
    sec = lax.axis_index("section")
    me = lax.axis_index("seq")
    return sec, me, (sec // 2) * 2, sec % 2, me // 4, me % 4


def plane_barrier(outside):
    sec, me, base, core, z, y = place()
    barrier = pltpu.get_barrier_semaphore()
    mine = core * 32 + me

    def greet(step, carry):
        other = (mine + step) % 64
        pl.semaphore_signal(
            barrier, inc=1, device_id=(base + other // 32, other % 32), device_id_type=MESH
        )
        return carry

    lax.fori_loop(1, 64, greet, 0)
    if outside:
        pl.semaphore_signal(
            barrier, inc=1, device_id=((sec + 2 * core + 7) % 8, me), device_id_type=MESH
        )
    pl.semaphore_wait(barrier, 64 if outside else 63)


def forward_kernel(
    q, k, v, grad_hbm, weight_hbm, rank_row, tiles,
    comp, tab, local_q, local_k, local_v, carry_in,
    halo_k, halo_v, grad_heads, carry_grad, score, dprob, flip, total_k, total_v,
    grad_in, weight, dense, mid0, mid1, mid2, mid3, pick, spread, arr0, arr1, arr2, arr3, counts, table,
    send_count, recv_count, send_grad, recv_grad, weight_sem, send_one, recv_one, send_two, recv_two,
    send_halo, recv_halo, table_sem, send_carry, recv_carry,
):
    sec, me, base, core, z, y = place()
    seat = y * 2 + core
    parity = z % 2
    mid = (mid0, mid1, mid2, mid3)
    arrived = (arr0, arr1, arr2, arr3)
    get_weight = pltpu.make_async_copy(weight_hbm, weight, weight_sem)
    get_weight.start()
    plane_barrier(True)

    def count_copy(n):
        plane = 2 * (n // 8) + core
        dest_section = base + n % 2
        dest = plane * 4 + (n % 8) // 2
        own = (dest_section == sec) & (dest == me)
        copy = remote(
            tiles.at[n // 8], counts.at[me], send_count.at[n], recv_count, (dest_section, dest)
        )
        return own, copy

    def send_counts(n, carry):
        own, copy = count_copy(n)

        @pl.when(own)
        def _():
            pltpu.make_async_copy(tiles.at[n // 8], counts.at[me], recv_count).start()

        @pl.when(jnp.logical_not(own))
        def _():
            copy.start()

        return carry

    lax.fori_loop(0, 32, send_counts, 0)
    grad_copy = remote(grad_hbm, grad_in, send_grad, recv_grad, ((sec + 7) % 8, me))
    grad_copy.start()
    after = (sec, (me + 1) % 32)
    halo_copies = [
        remote(src.at[:, pl.ds(512, 512)], dst, send_halo.at[n], recv_halo.at[n], after)
        for n, (src, dst) in enumerate(((k, halo_k), (v, halo_v)))
    ]

    carry_copies = [
        remote(
            carry_grad.at[pl.ds(2 * n, 2)], carry_in.at[pl.ds(2 * n, 2)],
            send_carry.at[n], recv_carry.at[n], (sec, (me + 31) % 32),
        )
        for n in range(2)
    ]

    def one_copy(t, h):
        return remote(
            dense.at[t, h], mid[t].at[z // 2], send_one.at[t, h], recv_one.at[t, z // 2],
            (base + parity, (2 * h + core) * 4 + y),
        )

    def start_one(t, h):
        own = (2 * h + core) == z

        @pl.when(own)
        def _():
            pltpu.make_async_copy(dense.at[t, h], mid[t].at[z // 2], recv_one.at[t, z // 2]).start()

        @pl.when(jnp.logical_not(own))
        def _():
            one_copy(t, h).start()

    rows = lax.broadcasted_iota(I32, (512, 512), 0)
    for h in range(HR):
        pick[h] = jnp.where(rows == rank_row[h : h + 1, :], 1.0, 0.0).astype(BF)
    for t, src in enumerate((k, v, q)):
        for h in range(HR):
            rowsh = jnp.dot(pick[h], src[:, h * HD : (h + 1) * HD], preferred_element_type=F32)
            dense[t, h] = rowsh.astype(BF).reshape(32, 16, HD)
            start_one(t, h)
        if t == 0:
            for copy in halo_copies:
                copy.start()

    pltpu.make_async_copy(counts, counts, recv_count).wait()
    tab[0:32, :] = counts[:, 1, :]
    tab[72:104, :] = counts[:, 2, :]
    unit = counts[:, 0, :].astype(F32)
    below = (
        lax.broadcasted_iota(I32, (32, 32), 0) >= lax.broadcasted_iota(I32, (32, 32), 1)
    ).astype(F32)
    ends = jnp.dot(below, unit, preferred_element_type=F32)
    lane = lax.broadcasted_iota(I32, (32, 128), 1)
    mine = lane == seat
    my_end = jnp.sum(jnp.where(mine, ends, 0.0), axis=1, keepdims=True)
    my_unit = jnp.sum(jnp.where(mine, unit, 0.0), axis=1, keepdims=True)
    tab[32:64, :] = jnp.broadcast_to(my_end - my_unit, (32, 128)).astype(I32)
    passed = jnp.broadcast_to(my_end, (32, 128)) <= lane.astype(F32)
    source = jnp.sum(jnp.where(passed, 1.0, 0.0), axis=0, keepdims=True).astype(I32)
    begin = jnp.sum(jnp.where(passed, my_unit, 0.0), axis=0, keepdims=True).astype(I32)
    inside = lax.broadcasted_iota(I32, (1, 128), 1) - begin
    sz = source >> 2
    address = ((source & 3) * 2 + (sz & 1)) * 28 + (sz >> 1) * 7 + inside
    tab[64:72, :] = jnp.broadcast_to(address, (8, 128))
    table_copy = pltpu.make_async_copy(tab, table, table_sem)
    table_copy.start()
    table_copy.wait()

    def two_copy(t, d):
        c = (seat + d) % 8
        return remote(
            spread.at[t, d], arrived[t].at[pl.ds(seat * 28, 28)], send_two.at[t, d],
            recv_two.at[t, seat], (base + c % 2, z * 4 + c // 2),
        )

    def second_stage(t):
        for slot in range(4):
            remote(
                mid[t].at[slot], mid[t].at[slot], send_one.at[t, 0], recv_one.at[t, slot], (sec, me)
            ).wait_recv()

        def expand(d):
            c = (seat + d) % 8
            for slot in range(4):
                first = table[(slot * 2 + core) * 4 + y, c]
                for r in range(7):
                    spread[t, d, slot * 7 + r] = mid[t][slot, jnp.clip(first + r, 0, 31)]

        def step(d, carry):
            expand(d)
            two_copy(t, d).start()
            return carry

        lax.fori_loop(1, 8, step, 0)
        expand(0)
        pltpu.make_async_copy(
            spread.at[t, 0], arrived[t].at[pl.ds(seat * 28, 28)], recv_two.at[t, seat]
        ).start()

    second_stage(0)
    grad_copy.wait_recv()
    get_weight.wait()

    def project(n, carry):
        part = lax.dot_general(
            grad_in[...], weight[pl.ds(pl.multiple_of(n * 256, 256), 256), :], NT,
            preferred_element_type=F32,
        ).astype(BF)
        grad_heads[2 * n] = part[:, :HD]
        grad_heads[2 * n + 1] = part[:, HD:]
        return carry

    lax.fori_loop(0, 4, project, 0)
    for h in range(HR):
        rowsh = jnp.dot(pick[h], grad_heads[h], preferred_element_type=F32)
        dense[3, h] = rowsh.astype(BF).reshape(32, 16, HD)
        start_one(3, h)
    second_stage(1)
    low = lax.broadcasted_iota(I32, (256, 256), 0)
    col = lax.broadcasted_iota(I32, (256, 256), 1)
    behind = jnp.broadcast_to(me > 0, (256, 256))

    def local_head(h, carry):
        cols = pl.ds(pl.multiple_of((h + 4) * HD, HD), HD)
        half = pl.ds(pl.multiple_of(h * HD, HD), HD)

        def key_rows(n, halo, own):
            if n < 2:
                return halo[n * 256 : (n + 1) * 256, half]
            return own[(n - 2) * 256 : (n - 1) * 256, cols]

        for n in range(4):
            flip[n] = jnp.transpose(key_rows(n, halo_k, k).astype(F32)).astype(BF)
        total_k[...] = jnp.zeros_like(total_k)
        total_v[...] = jnp.zeros_like(total_v)
        for blk in range(2):
            rows = slice(blk * 256, (blk + 1) * 256)
            masks = [low > col, None, low <= col]
            for n in range(3):
                if blk + n < 2:
                    masks[n] = behind if masks[n] is None else masks[n] & behind

            def add(n, dk, dv, blk=blk):
                spot = slice((blk + n) * 256, (blk + n + 1) * 256)
                total_k[spot, :] += dk
                total_v[spot, :] += dv

            local_q[h, rows, :] = attend(
                score, dprob, q[rows, cols], grad_heads[4 + h, rows, :],
                lambda n: key_rows(blk + n, halo_k, k),
                lambda n: key_rows(blk + n, halo_v, v),
                lambda n: flip[blk + n],
                masks, add,
            )
        carry_grad[h, 0] = (total_k[0:512, :] * FACTOR).astype(BF)
        carry_grad[h, 1] = total_v[0:512, :].astype(BF)
        local_k[h] = total_k[512:1024, :] * FACTOR
        local_v[h] = total_v[512:1024, :]
        return carry

    for copy in halo_copies:
        copy.wait_recv()
    lax.fori_loop(0, 2, local_head, 0)
    carry_copies[0].start()
    second_stage(2)
    lax.fori_loop(2, 4, local_head, 0)
    carry_copies[1].start()
    second_stage(3)
    for t in range(4):
        def await_two(j, carry, t=t):
            region = arrived[t].at[pl.ds(j * 28, 28)]
            remote(region, region, send_two.at[t, 0], recv_two.at[t, j], (sec, me)).wait_recv()
            return carry

        lax.fori_loop(0, 8, await_two, 0)

        def gather(n, carry, t=t):
            for m in range(8):
                comp[t, n * 8 + m] = arrived[t][jnp.clip(table[64, n * 8 + m], 0, 223)]
            return carry

        lax.fori_loop(0, 16, gather, 0)
    for copy in halo_copies:
        copy.wait_send()
    for copy in carry_copies:
        copy.wait()
    grad_copy.wait_send()

    def drain_counts(n, carry):
        own, copy = count_copy(n)

        @pl.when(jnp.logical_not(own))
        def _():
            copy.wait_send()

        return carry

    lax.fori_loop(0, 32, drain_counts, 0)
    for t in range(4):
        for h in range(HR):
            @pl.when((2 * h + core) != z)
            def _(t=t, h=h):
                one_copy(t, h).wait_send()

        def drain_two(d, carry, t=t):
            two_copy(t, d).wait_send()
            return carry

        lax.fori_loop(1, 8, drain_two, 0)


def return_kernel(
    answer, table,
    back,
    spread, arr0, arr1, arr2, dense,
    send_one, recv_one, send_two, recv_two,
):
    sec, me, base, core, z, y = place()
    seat = y * 2 + core
    arrived = (arr0, arr1, arr2)
    plane_barrier(False)

    def one_copy(t, d):
        j = (seat + d) % 8
        return remote(
            spread.at[t, d], arrived[t].at[pl.ds(seat * 28, 28)], send_one.at[t, d],
            recv_one.at[t, seat], (base + j % 2, z * 4 + j // 2),
        )

    def expand(t, d):
        j = (seat + d) % 8
        for slot in range(4):
            first = table[32 + (slot * 2 + j % 2) * 4 + j // 2, 0]
            for r in range(7):
                spread[t, d, slot * 7 + r] = answer[t, jnp.clip(first + r, 0, 127)]

    for t in range(3):
        def step(d, carry, t=t):
            expand(t, d)
            one_copy(t, d).start()
            return carry

        lax.fori_loop(1, 8, step, 0)
        expand(t, 0)
        pltpu.make_async_copy(
            spread.at[t, 0], arrived[t].at[pl.ds(seat * 28, 28)], recv_one.at[t, seat]
        ).start()

    def two_copy(t, slot):
        return remote(
            dense.at[t, slot], back.at[t, z // 2], send_two.at[t, slot], recv_two.at[t, z // 2],
            (base + z % 2, (slot * 2 + core) * 4 + y),
        )

    def own_slot(slot):
        return ((slot * 2 + core) == z) & (z % 2 == core)

    for t in range(3):
        def await_one(j, carry, t=t):
            region = arrived[t].at[pl.ds(j * 28, 28)]
            remote(region, region, send_one.at[t, 0], recv_one.at[t, j], (sec, me)).wait_recv()
            return carry

        lax.fori_loop(0, 8, await_one, 0)
        for slot in range(4):
            row = 72 + (slot * 2 + core) * 4 + y

            def gather(n, carry, t=t, slot=slot, row=row):
                for m in range(8):
                    dense[t, slot, n * 8 + m] = arrived[t][jnp.clip(table[row, n * 8 + m] + slot * 7, 0, 223)]
                return carry

            lax.fori_loop(0, 4, gather, 0)

            @pl.when(own_slot(slot))
            def _(t=t, slot=slot):
                pltpu.make_async_copy(
                    dense.at[t, slot], back.at[t, z // 2], recv_two.at[t, z // 2]
                ).start()

            @pl.when(jnp.logical_not(own_slot(slot)))
            def _(t=t, slot=slot):
                two_copy(t, slot).start()

    for t in range(3):
        for h in range(HR):
            remote(
                back.at[t, h], back.at[t, h], send_two.at[t, 0], recv_two.at[t, h], (sec, me)
            ).wait_recv()
    for t in range(3):
        def drain(d, carry, t=t):
            one_copy(t, d).wait_send()
            return carry

        lax.fori_loop(1, 8, drain, 0)
        for slot in range(4):
            @pl.when(jnp.logical_not(own_slot(slot)))
            def _(t=t, slot=slot):
                two_copy(t, slot).wait_send()


def block_rows(ref, index, first, count):
    return ref[index, pl.ds(first, count), :]


def attend(score, dprob, q_blk, g_blk, key_of, value_of, flip_of, masks, add):
    count = len(masks)
    top = None
    for n in range(count):
        s = lax.dot_general(key_of(n), q_blk, NT, preferred_element_type=F32) * FACTOR
        if masks[n] is not None:
            s = jnp.where(masks[n], s, -1e30)
        score[n] = s
        high = jnp.max(s, axis=0, keepdims=True)
        top = high if top is None else jnp.maximum(top, high)
    total = jnp.zeros((1, 256), F32)
    cross = jnp.zeros((1, 256), F32)
    for n in range(count):
        e = jnp.exp(score[n] - top)
        dp = lax.dot_general(value_of(n), g_blk, NT, preferred_element_type=F32)
        score[n] = e
        dprob[n] = dp
        total = total + jnp.sum(e, axis=0, keepdims=True)
        cross = cross + jnp.sum(e * dp, axis=0, keepdims=True)
    inverse = 1.0 / total
    delta = cross * inverse
    flipped = jnp.zeros((HD, 256), F32)
    for n in range(count):
        prob = score[n] * inverse
        ds = (prob * (dprob[n] - delta)).astype(BF)
        add(n, jnp.dot(ds, q_blk, preferred_element_type=F32),
            jnp.dot(prob.astype(BF), g_blk, preferred_element_type=F32))
        flipped = flipped + jnp.dot(flip_of(n), ds, preferred_element_type=F32)
    return (jnp.transpose(flipped) * FACTOR).astype(BF)


def compute_kernel(
    comp,
    answer,
    score, dprob, flip, total_k, total_v,
):
    low = lax.broadcasted_iota(I32, (256, 256), 0)
    col = lax.broadcasted_iota(I32, (256, 256), 1)
    total_k[...] = jnp.zeros_like(total_k)
    total_v[...] = jnp.zeros_like(total_v)
    for n in range(8):
        flip[n] = jnp.transpose(comp[0, n * 256 : (n + 1) * 256, :].astype(F32)).astype(BF)
    causal = low <= col
    for blk in range(7, -1, -1):
        rows = slice(blk * 256, (blk + 1) * 256)

        def add(n, dk, dv):
            total_k[n * 256 : (n + 1) * 256, :] += dk
            total_v[n * 256 : (n + 1) * 256, :] += dv

        answer[2, rows, :] = attend(
            score, dprob, comp[2, rows, :], comp[3, rows, :],
            lambda n: comp[0, n * 256 : (n + 1) * 256, :],
            lambda n: comp[1, n * 256 : (n + 1) * 256, :],
            lambda n: flip[n],
            [None] * blk + [causal], add,
        )
        answer[0, rows, :] = (total_k[rows, :] * FACTOR).astype(BF)
        answer[1, rows, :] = total_v[rows, :].astype(BF)


def finish_kernel(back, carry_in, rank_col, local_q, local_k, local_v, out_q, out_k, out_v):
    keep = lax.axis_index("seq") < 31
    cols = lax.broadcasted_iota(I32, (512, 512), 1)
    for h in range(HR):
        place_rows = jnp.where(cols == rank_col[:, h : h + 1], 1.0, 0.0).astype(BF)
        span = slice(h * HD, (h + 1) * HD)
        for t, out in enumerate((out_k, out_v, out_q)):
            out[:, span] = jnp.dot(place_rows, back[t, h], preferred_element_type=F32).astype(BF)
        span = slice((h + 4) * HD, (h + 5) * HD)
        out_q[:, span] = local_q[h]
        for t, (out, local) in enumerate(((out_k, local_k), (out_v, local_v))):
            extra = jnp.where(keep, carry_in[h, t].astype(F32), 0.0)
            out[:, span] = (local[h] + extra).astype(BF)


VM = pl.BlockSpec(memory_space=pltpu.VMEM)
SM = pl.BlockSpec(memory_space=pltpu.SMEM)
HBM = pl.BlockSpec(memory_space=pl.ANY)
SDS = jax.ShapeDtypeStruct
DMA = pltpu.SemaphoreType.DMA


def plan(labels):
    members = (labels[:, :, None] == jnp.arange(8, dtype=I32)[None, None, :]).astype(BF)
    ids = jnp.arange(512, dtype=I32)
    lower = (ids[:, None] >= ids[None, :]).astype(BF)
    running = jnp.einsum("ts,hsc->htc", lower, members, preferred_element_type=F32)
    counts = running[:, -1, :].astype(I32)
    clusters = jnp.arange(8, dtype=I32)
    ends = jnp.sum(jnp.where(clusters[:, None] <= clusters[None, :], counts[:, :, None], 0), axis=1)
    starts = ends - counts
    offset = running - 1.0 + starts.astype(F32)[:, None, :]
    ranks = jnp.sum(jnp.where(members > 0, offset, 0.0), axis=2).astype(I32)
    units, unit_start, unit_end = counts // 16, starts // 16, ends // 16
    lanes = jnp.arange(128, dtype=I32)
    passed = unit_end[:, :, None] <= lanes[None, None, :]
    which = jnp.sum(passed.astype(I32), axis=1)
    begun = jnp.sum(jnp.where(passed, units[:, :, None], 0), axis=1)
    inverse = jnp.where(lanes < 32, which * 28 + lanes - begun, 0)
    wide = lambda x: jnp.pad(x, ((0, 0), (0, 120)))
    zero = jnp.zeros_like(inverse)
    tiles = jnp.stack([wide(units), wide(unit_start), inverse] + [zero] * 5, axis=1)
    return ranks, tiles


def body(query, key, value, grad_sent, out_weight, assign):
    ranks, tiles = plan(assign[0])
    rank_row = jnp.pad(ranks, ((0, 4), (0, 0)))
    rank_col = rank_row.T
    q, k, v = query[0], key[0], value[0]
    comp, tab, local_q, local_k, local_v, carry_in = pl.pallas_call(
        forward_kernel,
        out_shape=(
            SDS((4, 128, 16, HD), BF), SDS((104, 128), I32), SDS((4, 512, HD), BF),
            SDS((4, 512, HD), F32), SDS((4, 512, HD), F32), SDS((4, 2, 512, HD), BF),
        ),
        in_specs=[VM, VM, VM, HBM, HBM, VM, VM],
        out_specs=(VM,) * 6,
        scratch_shapes=[
            pltpu.VMEM((512, 512), BF), pltpu.VMEM((512, 512), BF), pltpu.VMEM((8, 512, HD), BF),
            pltpu.VMEM((4, 2, 512, HD), BF), pltpu.VMEM((3, 256, 256), F32),
            pltpu.VMEM((3, 256, 256), F32), pltpu.VMEM((4, HD, 256), BF),
            pltpu.VMEM((1024, HD), F32), pltpu.VMEM((1024, HD), F32),
            pltpu.VMEM((512, 2048), BF), pltpu.VMEM((1024, 2048), BF),
            pltpu.VMEM((4, 4, 32, 16, HD), BF), *[pltpu.VMEM((4, 32, 16, HD), BF)] * 4,
            pltpu.VMEM((4, 512, 512), BF), pltpu.VMEM((4, 8, 28, 16, HD), BF),
            *[pltpu.VMEM((224, 16, HD), BF)] * 4, pltpu.VMEM((32, 8, 128), I32),
            pltpu.SMEM((104, 128), I32),
            DMA((32,)), DMA, DMA, DMA, DMA, DMA((4, 4)), DMA((4, 4)), DMA((4, 8)), DMA((4, 8)),
            DMA((2,)), DMA((2,)), DMA, DMA((2,)), DMA((2,)),
        ],
        compiler_params=pltpu.CompilerParams(collective_id=0, has_side_effects=True),
        name="exchange_forward",
    )(q, k, v, grad_sent[0], out_weight[0], rank_row, tiles)
    answer = pl.pallas_call(
        compute_kernel,
        out_shape=SDS((3, 2048, HD), BF),
        in_specs=[VM],
        out_specs=VM,
        scratch_shapes=[
            pltpu.VMEM((8, 256, 256), F32), pltpu.VMEM((8, 256, 256), F32),
            pltpu.VMEM((8, HD, 256), BF), pltpu.VMEM((2048, HD), F32), pltpu.VMEM((2048, HD), F32),
        ],
        name="attention_backward",
    )(comp.reshape(4, 2048, HD))
    back = pl.pallas_call(
        return_kernel,
        out_shape=SDS((3, 4, 32, 16, HD), BF),
        in_specs=[VM, SM],
        out_specs=VM,
        scratch_shapes=[
            pltpu.VMEM((3, 8, 28, 16, HD), BF), *[pltpu.VMEM((224, 16, HD), BF)] * 3,
            pltpu.VMEM((3, 4, 32, 16, HD), BF),
            DMA((3, 8)), DMA((3, 8)), DMA((3, 4)), DMA((3, 4)),
        ],
        compiler_params=pltpu.CompilerParams(collective_id=1, has_side_effects=True),
        name="exchange_return",
    )(answer.reshape(3, 128, 16, HD), tab)
    outs = pl.pallas_call(
        finish_kernel,
        out_shape=(SDS((512, 1024), BF),) * 3,
        in_specs=[VM] * 6,
        out_specs=(VM,) * 3,
        name="finish",
    )(back.reshape(3, 4, 512, HD), carry_in, rank_col, local_q, local_k, local_v)
    return tuple(out[None] for out in outs)


def solution(mesh):
    return jax.shard_map(
        body,
        mesh=mesh,
        in_specs=(P("section", "seq", None),) * 4
        + (P("section", None, None), P("section", None, "seq")),
        out_specs=(P("section", "seq", None),) * 3,
        check_vma=False,
    )
```
